128 devices in a mesh: src: 4 (over x_lo, core), tgt: 32 (over y, x_hi, z).
Axes of the slice: x: 4 (x_hi: 2, x_lo: 2; x = x_hi * 2 + x_lo), y: 4, z: 4, core: 2. Of those that a mesh axis runs over, the one named last changes fastest.
Arguments:
- source_feat: bfloat16 [16384, 256], P(('src', 'tgt')), may hold values from -40 to 40
- target_feat: bfloat16 [57600, 256], P('tgt', 'src'), may hold values from -4 to 4
- proj: bfloat16 [256, 256], replicated, may hold values from -0.375 to 0.375
Outputs:
- flow: float32 [2, 16384], P(None, ('src', 'tgt'))
- matched: bfloat16 [16384, 256], P(('src', 'tgt'))
The draws below stay inside these ranges and needn't reach their ends.
All inputs are finite; a program needn't handle non-finite values.
Results may differ from the reference program's by a relative error of at most 0.0075.
Values may be sent and summed in bfloat16 or wider, within the bound.
A program may use at most 256 MiB of HBM per device.

```python
import math
import jax
import jax.numpy as jnp
from jax import lax

C = 256
W_GRID = 320
SOURCES = 16384
TARGETS = 57600


def target_table(key):
    base = jax.random.fold_in(key, 11)
    table = jnp.clip(jax.random.normal(base, (TARGETS, C), jnp.float32), -4.0, 4.0)
    return table


def draw_target_feat(key, part):
    return target_table(key).astype(jnp.bfloat16)


def draw_source_feat(key, part):
    scale_key = jax.random.fold_in(key, 23)
    value_key = jax.random.fold_in(key, 37)
    row_scale = jnp.exp(jax.random.uniform(scale_key, (SOURCES,), jnp.float32, math.log(0.3), math.log(2.0)))
    values = jnp.clip(jax.random.normal(value_key, (SOURCES, C), jnp.float32), -6.0, 6.0) * row_scale[:, None]
    return values.astype(jnp.bfloat16)


def scatter_about(own_key, dims, deviation, most, kind=jnp.bfloat16):
    array = deviation * jax.random.normal(own_key, dims, jnp.float32)
    return jnp.clip(array, min=-most, max=most).astype(kind)


def setup_inputs(seed: int = 0) -> dict:
    key_list = jax.random.split(jax.random.key(seed), 4)
    return {
        "source_feat": draw_source_feat(jax.random.fold_in(key_list[3], 71), 0),
        "target_feat": draw_target_feat(jax.random.fold_in(key_list[3], 71), 0),
        "proj": scatter_about(key_list[2], (C, C), C ** -0.5, 0.375),
    }


def reference(source_feat, target_feat, proj):
    queries = jnp.dot(source_feat, proj, preferred_element_type=jnp.float32).astype(jnp.bfloat16)
    keys = jnp.dot(target_feat, proj, preferred_element_type=jnp.float32).astype(jnp.bfloat16)
    width = queries.shape[1]
    count = keys.shape[0]
    pos = jnp.arange(count, dtype=jnp.int32)
    grid_x = (pos % W_GRID).astype(jnp.float32) / W_GRID
    grid_y = (pos // W_GRID).astype(jnp.float32) / W_GRID
    rows = queries.shape[0]
    block = min(256, rows)
    blocks = queries.reshape(rows // block, block, width)

    def one_block(qblock):
        scores = jnp.einsum("qc,kc->qk", qblock, keys, preferred_element_type=jnp.float32) * (width ** -0.5)
        top = jnp.max(scores, axis=1)
        weights = jnp.exp(scores - top[:, None])
        total = jnp.sum(weights, axis=1)
        coord_x = jnp.sum(weights * grid_x[None, :], axis=1)
        coord_y = jnp.sum(weights * grid_y[None, :], axis=1)
        feat_sum = jnp.dot(weights.astype(jnp.bfloat16), keys, preferred_element_type=jnp.float32)
        return total, coord_x, coord_y, feat_sum

    total, coord_x, coord_y, feat_sum = lax.map(one_block, blocks)
    total = total.reshape(rows)
    coord_x = coord_x.reshape(rows)
    coord_y = coord_y.reshape(rows)
    feat_sum = feat_sum.reshape(rows, width)
    own = jnp.arange(rows, dtype=jnp.int32)
    own_x = (own % W_GRID).astype(jnp.float32) / W_GRID
    own_y = (own // W_GRID).astype(jnp.float32) / W_GRID
    flow = jnp.stack([coord_x / total - own_x, coord_y / total - own_y], axis=0)
    matched = (feat_sum / total[:, None]).astype(jnp.bfloat16)
    return flow, matched
```

```python
import jax
import jax.numpy as jnp
from jax import lax
from jax.experimental import pallas as pl
from jax.experimental.pallas import tpu as pltpu
from jax.sharding import PartitionSpec as P

MESH = pl.DeviceIdType.MESH
W_GRID = 320
C = 256
ROWS = 128
STRIP = 1800
HALF = 912
DUP = 2 * HALF - STRIP
KEYS = 4 * HALF
GROUP = 16
PAIRS = GROUP // 2
AUG = 16
F32 = jnp.float32
BF16 = jnp.bfloat16
NT = (((1,), (1,)), ((), ()))


def place():
    s, t = lax.axis_index("src"), lax.axis_index("tgt")
    return (t // 4 % 2) * 2 + s // 2, t // 8, t % 4, s % 2


def device(x, y, z, c):
    return ((x % 2) * 2 + c, (y * 2 + x // 2) * 4 + z)


def grid_of(pos):
    gy = jnp.floor((pos + 0.5) * (1.0 / W_GRID))
    return pos - gy * W_GRID, gy


def kernel(
    src_ref,
    tgt_ref,
    proj_ref,
    flow_ref,
    matched_ref,
    w_ref,
    pack,
    qbuf,
    keys,
    keys_t,
    s0,
    s1,
    m0,
    m1,
    stage,
    sstage,
    rbuf,
    rstat,
    p_send,
    p_recv,
    f_send,
    f_recv,
    q_send,
    q_recv,
    o_send,
    o_recv,
    t_send,
    t_recv,
):
    x, y, z, c = place()

    def yz(i, sign):
        j = (i + 1) % GROUP
        return device(x, (y + sign * (j // 4) + 4) % 4, (z + sign * (j % 4) + 4) % 4, c)

    sibling = device(x, y, z, 1 - c)

    barrier = pltpu.get_barrier_semaphore()

    def greet(i, carry):
        pl.semaphore_signal(barrier, inc=1, device_id=yz(i, 1), device_id_type=MESH)
        return carry

    lax.fori_loop(0, GROUP - 1, greet, 0)
    for k in range(1, 4):
        pl.semaphore_signal(
            barrier, inc=1, device_id=device((x + k) % 4, y, z, c), device_id_type=MESH
        )
    pl.semaphore_signal(barrier, inc=1, device_id=sibling, device_id_type=MESH)

    def slot_of(xx, cc):
        return (xx // 2) * 4 + (xx % 2) * 2 + cc

    own = slot_of(x, c)
    e_row = lax.broadcasted_iota(jnp.int32, (64, 128), 0)
    e_col = lax.broadcasted_iota(jnp.int32, (64, 128), 1)
    t32 = tgt_ref[...].astype(F32)
    packed = jnp.dot(
        t32[:HALF].astype(BF16), (e_row == e_col).astype(BF16), preferred_element_type=F32
    ) + jnp.dot(
        t32[STRIP - HALF :].astype(BF16),
        (e_row + 64 == e_col).astype(BF16),
        preferred_element_type=F32,
    )
    pack[own] = packed.astype(BF16)
    queries = jnp.dot(src_ref[...], proj_ref[...], preferred_element_type=F32).astype(BF16)
    own_q = pl.ds((GROUP - 1) * ROWS, ROWS)
    qbuf[own_q, :] = (queries.astype(F32) * (1.0 / 16.0)).astype(BF16)

    pl.semaphore_wait(barrier, GROUP - 1 + 4)

    def key_copy(k):
        return pltpu.make_async_remote_copy(
            src_ref=pack.at[own],
            dst_ref=pack.at[own],
            send_sem=p_send.at[k],
            recv_sem=p_recv.at[k],
            device_id=device((x + k) % 4, y, z, c),
            device_id_type=MESH,
        )

    def key_arrival(k):
        slot = slot_of((x - k + 4) % 4, c)
        return pltpu.make_async_remote_copy(
            src_ref=pack.at[slot],
            dst_ref=pack.at[slot],
            send_sem=p_send.at[k],
            recv_sem=p_recv.at[k],
            device_id=device((x - k + 4) % 4, y, z, c),
            device_id_type=MESH,
        )

    def forward(k):
        slot = slot_of((x - k + 4) % 4, c)
        return pltpu.make_async_remote_copy(
            src_ref=pack.at[slot],
            dst_ref=pack.at[slot],
            send_sem=f_send.at[k],
            recv_sem=f_recv.at[k],
            device_id=sibling,
            device_id_type=MESH,
        )

    def forward_arrival(k):
        slot = slot_of((x - k + 4) % 4, 1 - c)
        return pltpu.make_async_remote_copy(
            src_ref=pack.at[slot],
            dst_ref=pack.at[slot],
            send_sem=f_send.at[k],
            recv_sem=f_recv.at[k],
            device_id=sibling,
            device_id_type=MESH,
        )

    def query_copy(i):
        return pltpu.make_async_remote_copy(
            src_ref=qbuf.at[own_q],
            dst_ref=qbuf.at[pl.ds(pl.multiple_of(i * ROWS, ROWS), ROWS)],
            send_sem=q_send.at[i],
            recv_sem=q_recv.at[i],
            device_id=yz(i, -1),
            device_id_type=MESH,
        )

    def feat_copy(i):
        return pltpu.make_async_remote_copy(
            src_ref=stage.at[i],
            dst_ref=rbuf.at[i],
            send_sem=o_send.at[i],
            recv_sem=o_recv.at[i],
            device_id=yz(i, 1),
            device_id_type=MESH,
        )

    def stat_copy(i):
        return pltpu.make_async_remote_copy(
            src_ref=sstage.at[i],
            dst_ref=rstat.at[i],
            send_sem=t_send.at[i],
            recv_sem=t_recv.at[i],
            device_id=yz(i, 1),
            device_id_type=MESH,
        )

    for k in (1, 3, 2):
        key_copy(k).start()
    forward(0).start()

    def send_query(i, carry):
        query_copy(i).start()
        return carry

    lax.fori_loop(0, GROUP - 1, send_query, 0)

    w_ref[...] = jnp.zeros_like(w_ref)
    for d in range(4):
        rows = proj_ref[d * 64 : (d + 1) * 64, :]
        w_ref[d * 128 : d * 128 + 64, 0:C] = rows
        w_ref[d * 128 + 64 : (d + 1) * 128, C : 2 * C] = rows
    col = lax.broadcasted_iota(jnp.int32, (1, KEYS), 1)
    second = (col >= 2 * HALF).astype(jnp.int32)
    half = col - 2 * HALF * second
    right = (half >= HALF).astype(jnp.int32)
    valid = (half < HALF) | (half >= HALF + DUP)
    base = ((y * 2) * 4 + z) * STRIP
    pos = base + second * (4 * STRIP) + half - DUP * right
    kx, ky = grid_of(pos.astype(F32))
    kxh = jnp.floor(kx * (1.0 / 16.0))
    kxl = kx - 16.0 * kxh
    row = lax.broadcasted_iota(jnp.int32, (AUG, KEYS), 0)
    aug = jnp.where(
        row == 0, 1.0, jnp.where(row == 1, kxh, jnp.where(row == 2, kxl, jnp.where(row == 3, ky, 0.0)))
    )
    keys_t[C : C + AUG, :] = jnp.where(valid, aug, 0.0).astype(BF16)

    for k in (1, 3, 2):
        key_arrival(k).wait_recv()
        forward(k).start()
    for k in range(4):
        forward_arrival(k).wait_recv()

    for s in range(2):
        cat = jnp.concatenate([pack[4 * s + d] for d in range(4)], axis=1)
        a = jnp.dot(cat, w_ref[...], preferred_element_type=F32).astype(BF16)
        keys[2 * s * HALF : (2 * s + 1) * HALF, :] = a[:, :C]
        keys[(2 * s + 1) * HALF : (2 * s + 2) * HALF, :] = a[:, C:]
    i_row = lax.broadcasted_iota(jnp.int32, (C, C), 0)
    i_col = lax.broadcasted_iota(jnp.int32, (C, C), 1)
    kt = lax.dot_general(
        (i_row == i_col).astype(BF16), keys[...], NT, preferred_element_type=F32
    )
    keys_t[0:C, :] = jnp.where(valid, kt, 0.0).astype(BF16)

    def match(p, s_ref, m_ref):
        for i in (2 * p, 2 * p + 1):

            @pl.when(i < GROUP - 1)
            def _():
                query_copy(i).wait_recv()

        q = qbuf[pl.ds(pl.multiple_of(p * 2 * ROWS, 2 * ROWS), 2 * ROWS), :]
        s = lax.dot_general(keys[...], q, NT, preferred_element_type=F32)
        s_ref[...] = s
        m_ref[...] = jnp.max(s, axis=0, keepdims=True)

    def gather(p, s_ref, m_ref):
        m = m_ref[...]
        w = jnp.exp(s_ref[...] - m).astype(BF16)
        o = jnp.dot(keys_t[...], w, preferred_element_type=F32)
        srow = lax.broadcasted_iota(jnp.int32, (8, 2 * ROWS), 0)
        stat = jnp.where(srow == 4, m, o[C : C + 8, :])
        for e in range(2):
            i = 2 * p + e
            lanes = slice(e * ROWS, (e + 1) * ROWS)
            stage[i] = o[:C, lanes].astype(BF16)
            sstage[i] = stat[:, lanes]

            @pl.when(i < GROUP - 1)
            def _():
                feat_copy(i).start()
                stat_copy(i).start()

    match(0, s0, m0)

    def steps(j, carry):
        p = 2 * j
        match(p + 1, s1, m1)
        gather(p, s0, m0)
        match(p + 2, s0, m0)
        gather(p + 1, s1, m1)
        return carry

    lax.fori_loop(0, PAIRS // 2 - 1, steps, 0)
    match(PAIRS - 1, s1, m1)
    gather(PAIRS - 2, s0, m0)
    gather(PAIRS - 1, s1, m1)

    def settle(i, carry):
        query_copy(i).wait_send()
        feat_copy(i).wait_send()
        stat_copy(i).wait_send()
        feat_copy(i).wait_recv()
        stat_copy(i).wait_recv()
        return carry

    for k in range(1, 4):
        key_copy(k).wait_send()
    for k in range(4):
        forward(k).wait_send()
    lax.fori_loop(0, GROUP - 1, settle, 0)

    rstat[GROUP - 1] = sstage[GROUP - 1]
    top = rstat[0, 4:5, :]
    for i in range(1, GROUP):
        top = jnp.maximum(top, rstat[i, 4:5, :])
    total = jnp.zeros((8, ROWS), F32)
    feats = jnp.zeros((C, ROWS), F32)
    for i in range(GROUP):
        f = jnp.exp(rstat[i, 4:5, :] - top)
        part = rbuf[i] if i < GROUP - 1 else stage[i]
        total = total + rstat[i] * f
        feats = feats + part.astype(F32) * f
    inv = 1.0 / total[0:1]
    s_idx, t_idx = lax.axis_index("src"), lax.axis_index("tgt")
    lane = lax.broadcasted_iota(jnp.int32, (1, ROWS), 1)
    ox, oy = grid_of(((s_idx * 32 + t_idx) * ROWS + lane).astype(F32))
    cx = (total[1:2] * 16.0 + total[2:3]) * inv
    cy = total[3:4] * inv
    flow_ref[0:1, :] = (cx - ox) * (1.0 / W_GRID)
    flow_ref[1:2, :] = (cy - oy) * (1.0 / W_GRID)
    matched_ref[...] = (feats * inv).T.astype(BF16)


def per_device(source_feat, target_feat, proj):
    dma = pltpu.SemaphoreType.DMA
    vmem = pl.BlockSpec(memory_space=pltpu.VMEM)
    return pl.pallas_call(
        kernel,
        out_shape=(
            jax.ShapeDtypeStruct((2, ROWS), F32),
            jax.ShapeDtypeStruct((ROWS, C), BF16),
        ),
        in_specs=[vmem] * 3,
        out_specs=[vmem] * 2,
        scratch_shapes=[
            pltpu.VMEM((512, 512), BF16),
            pltpu.VMEM((8, HALF, 128), BF16),
            pltpu.VMEM((GROUP * ROWS, C), BF16),
            pltpu.VMEM((KEYS, C), BF16),
            pltpu.VMEM((C + AUG, KEYS), BF16),
            pltpu.VMEM((KEYS, 2 * ROWS), F32),
            pltpu.VMEM((KEYS, 2 * ROWS), F32),
            pltpu.VMEM((1, 2 * ROWS), F32),
            pltpu.VMEM((1, 2 * ROWS), F32),
            pltpu.VMEM((GROUP, C, ROWS), BF16),
            pltpu.VMEM((GROUP, 8, ROWS), F32),
            pltpu.VMEM((GROUP, C, ROWS), BF16),
            pltpu.VMEM((GROUP, 8, ROWS), F32),
            dma((4,)),
            dma((4,)),
            dma((4,)),
            dma((4,)),
            dma((GROUP,)),
            dma((GROUP,)),
            dma((GROUP,)),
            dma((GROUP,)),
            dma((GROUP,)),
            dma((GROUP,)),
        ],
        compiler_params=pltpu.CompilerParams(
            collective_id=0, has_side_effects=True, vmem_limit_bytes=50 << 20
        ),
        name="match_kernel",
    )(source_feat, target_feat, proj)


def solution(mesh):
    in_specs = (P(("src", "tgt"), None), P("tgt", "src"), P())
    out_specs = (P(None, ("src", "tgt")), P(("src", "tgt"), None))
    return jax.shard_map(
        per_device, mesh=mesh, in_specs=in_specs, out_specs=out_specs, check_vma=False
    )
```

```python
import jax
import jax.numpy as jnp
from jax import lax
from jax.experimental import pallas as pl
from jax.experimental.pallas import tpu as pltpu
from jax.sharding import PartitionSpec as P

MESH = pl.DeviceIdType.MESH
W_GRID = 320
C = 256
ROWS = 128
STRIP = 1800
GROUP = 16
PAIRS = GROUP // 2
CROWS = 64
HCH = CROWS // 2
AUG = 16
F32 = jnp.float32
BF16 = jnp.bfloat16
NT = (((1,), (1,)), ((), ()))
TN = (((0,), (0,)), ((), ()))
OFFSETS = (
    (1, 2), (2, 1), (3, 2), (2, 3), (2, 2), (1, 1), (3, 3), (1, 3),
    (3, 1), (0, 2), (2, 0), (0, 1), (1, 0), (0, 3), (3, 0), (0, 0),
)


def table(which, half):
    return sum(OFFSETS[8 * half + k][which] * 4**k for k in range(8))


def offset(which, i):
    tab = jnp.where(i < 8, table(which, 0), table(which, 1))
    return lax.shift_right_logical(tab, 2 * (i % 8)) % 4


def place():
    s, t = lax.axis_index("src"), lax.axis_index("tgt")
    return (t // 4 % 2) * 2 + s // 2, t // 8, t % 4, s % 2


def device(x, y, z, c):
    return ((x % 2) * 2 + c, (y * 2 + x // 2) * 4 + z)


def grid_of(pos):
    gy = jnp.floor((pos + 0.5) * (1.0 / W_GRID))
    return pos - gy * W_GRID, gy


def kernel(
    src_ref,
    tgt_ref,
    proj_ref,
    flow_ref,
    matched_ref,
    chans,
    qbuf,
    keys,
    keys_t,
    scores,
    top_ref,
    stage,
    sstage,
    rbuf,
    rstat,
    p_send,
    p_recv,
    f_send,
    f_recv,
    q_send,
    q_recv,
    o_send,
    o_recv,
    t_send,
    t_recv,
):
    x, y, z, c = place()

    def yz(i, sign):
        dy, dz = offset(0, i), offset(1, i)
        return device(x, (y + sign * dy + 4) % 4, (z + sign * dz + 4) % 4, c)

    sibling = device(x, y, z, 1 - c)

    barrier = pltpu.get_barrier_semaphore()

    def greet(i, carry):
        pl.semaphore_signal(barrier, inc=1, device_id=yz(i, 1), device_id_type=MESH)
        return carry

    lax.fori_loop(0, GROUP - 1, greet, 0)
    left, right = device((x + 3) % 4, y, z, c), device((x + 1) % 4, y, z, c)
    for other in (left, right):
        pl.semaphore_signal(barrier, inc=1, device_id=other, device_id_type=MESH)
    pl.semaphore_signal(barrier, inc=1, device_id=sibling, device_id_type=MESH)

    def piece(dx, cc, start, size):
        xx = (x + dx) % 4
        first = ((xx % 2) * 2 + cc) * CROWS + start
        return chans.at[xx // 2, pl.ds(pl.multiple_of(first, HCH), size)]

    piece(0, c, 0, CROWS)[...] = tgt_ref[...]
    queries = jnp.dot(src_ref[...], proj_ref[...], preferred_element_type=F32).astype(BF16)
    own_q = pl.ds((GROUP - 1) * ROWS, ROWS)
    qbuf[own_q, :] = (queries.astype(F32) * (1.0 / 16.0)).astype(BF16)

    pl.semaphore_wait(barrier, GROUP - 1 + 3)

    ring = ((1, 0, 0), (-1, 0, 1), (1, 0, 1), (-1, 0, 0), (1, -1, 0), (-1, 1, 1))

    def ring_copy(k, arrival):
        step, owner, h = ring[k]
        ref = piece(owner - step * arrival + 4, c, h * HCH, HCH)
        return pltpu.make_async_remote_copy(
            src_ref=ref,
            dst_ref=ref,
            send_sem=p_send.at[k],
            recv_sem=p_recv.at[k],
            device_id=right if step == 1 else left,
            device_id_type=MESH,
        )

    def core_copy(k, arrival):
        cc = 1 - c if arrival else c
        if k == len(ring):
            ref = piece(0, cc, 0, CROWS)
        else:
            step, owner, h = ring[k]
            ref = piece(owner - step + 4, cc, h * HCH, HCH)
        return pltpu.make_async_remote_copy(
            src_ref=ref,
            dst_ref=ref,
            send_sem=f_send.at[k],
            recv_sem=f_recv.at[k],
            device_id=sibling,
            device_id_type=MESH,
        )

    def query_copy(i):
        return pltpu.make_async_remote_copy(
            src_ref=qbuf.at[own_q],
            dst_ref=qbuf.at[pl.ds(pl.multiple_of(i * ROWS, ROWS), ROWS)],
            send_sem=q_send.at[i],
            recv_sem=q_recv.at[i],
            device_id=yz(i, -1),
            device_id_type=MESH,
        )

    def feat_copy(i):
        return pltpu.make_async_remote_copy(
            src_ref=stage.at[i],
            dst_ref=rbuf.at[i],
            send_sem=o_send.at[i],
            recv_sem=o_recv.at[i],
            device_id=yz(i, 1),
            device_id_type=MESH,
        )

    def stat_copy(i):
        return pltpu.make_async_remote_copy(
            src_ref=sstage.at[i],
            dst_ref=rstat.at[i],
            send_sem=t_send.at[i],
            recv_sem=t_recv.at[i],
            device_id=yz(i, 1),
            device_id_type=MESH,
        )

    for k in range(4):
        ring_copy(k, False).start()
    core_copy(6, False).start()

    def send_query(i, carry):
        query_copy(i).start()
        return carry

    lax.fori_loop(0, GROUP - 1, send_query, 0)

    mine = x // 2
    col = lax.broadcasted_iota(jnp.int32, (1, STRIP), 1)
    row = lax.broadcasted_iota(jnp.int32, (AUG, STRIP), 0)
    for e in range(2):
        strip = mine if e == 0 else 1 - mine
        base = ((y * 2 + strip) * 4 + z) * STRIP
        kx, ky = grid_of((base + col).astype(F32))
        kxh = jnp.floor(kx * (1.0 / 16.0))
        kxl = kx - 16.0 * kxh
        aug = jnp.where(
            row == 0,
            1.0,
            jnp.where(row == 1, kxh, jnp.where(row == 2, kxl, jnp.where(row == 3, ky, 0.0))),
        )
        keys_t[e, C : C + AUG, :] = aug.astype(BF16)

    def project(e):
        block = chans[mine if e == 0 else 1 - mine]
        keys[e] = lax.dot_general(block, proj_ref[...], TN, preferred_element_type=F32).astype(BF16)
        keys_t[e, 0:C, :] = lax.dot_general(
            proj_ref[...], block, TN, preferred_element_type=F32
        ).astype(BF16)

    for k in range(2):
        ring_copy(k, True).wait_recv()
        ring_copy(k + 4, False).start()
        core_copy(k, False).start()
    for k in range(2, 4):
        ring_copy(k, True).wait_recv()
        core_copy(k, False).start()
    for k in (6, 0, 1, 2, 3):
        core_copy(k, True).wait_recv()
    project(0)
    for k in range(4, 6):
        ring_copy(k, True).wait_recv()
        core_copy(k, False).start()
    for k in range(4, 6):
        core_copy(k, True).wait_recv()
    project(1)

    def pair(p, carry):
        def match(_, inner):
            for i in (2 * p, 2 * p + 1):

                @pl.when(i < GROUP - 1)
                def _():
                    query_copy(i).wait_recv()

            q = qbuf[pl.ds(pl.multiple_of(p * 2 * ROWS, 2 * ROWS), 2 * ROWS), :]
            tops = []
            for e in range(2):
                s = lax.dot_general(keys[e], q, NT, preferred_element_type=F32)
                scores[e] = s
                tops.append(jnp.max(s, axis=0, keepdims=True))
            top_ref[...] = jnp.maximum(tops[0], tops[1])
            return inner

        def gather(_, inner):
            m = top_ref[...]
            o = jnp.zeros((C + AUG, 2 * ROWS), F32)
            for e in range(2):
                w = jnp.exp(scores[e] - m).astype(BF16)
                o = o + jnp.dot(keys_t[e], w, preferred_element_type=F32)
            srow = lax.broadcasted_iota(jnp.int32, (8, 2 * ROWS), 0)
            stat = jnp.where(srow == 4, m, o[C : C + 8, :])
            for e in range(2):
                i = 2 * p + e
                lanes = slice(e * ROWS, (e + 1) * ROWS)
                stage[i] = o[:C, lanes].astype(BF16)
                sstage[i] = stat[:, lanes]

                @pl.when(i < GROUP - 1)
                def _():
                    feat_copy(i).start()
                    stat_copy(i).start()

            return inner

        lax.fori_loop(p, p + 1, match, 0)
        lax.fori_loop(p, p + 1, gather, 0)
        return carry

    lax.fori_loop(0, PAIRS, pair, 0)

    def settle(i, carry):
        query_copy(i).wait_send()
        feat_copy(i).wait_send()
        stat_copy(i).wait_send()
        feat_copy(i).wait_recv()
        stat_copy(i).wait_recv()
        return carry

    for k in range(6):
        ring_copy(k, False).wait_send()
    for k in range(7):
        core_copy(k, False).wait_send()
    lax.fori_loop(0, GROUP - 1, settle, 0)

    rstat[GROUP - 1] = sstage[GROUP - 1]
    top = rstat[0, 4:5, :]
    for i in range(1, GROUP):
        top = jnp.maximum(top, rstat[i, 4:5, :])
    total = jnp.zeros((8, ROWS), F32)
    feats = jnp.zeros((C, ROWS), F32)
    for i in range(GROUP):
        f = jnp.exp(rstat[i, 4:5, :] - top)
        part = rbuf[i] if i < GROUP - 1 else stage[i]
        total = total + rstat[i] * f
        feats = feats + part.astype(F32) * f
    inv = 1.0 / total[0:1]
    s_idx, t_idx = lax.axis_index("src"), lax.axis_index("tgt")
    lane = lax.broadcasted_iota(jnp.int32, (1, ROWS), 1)
    ox, oy = grid_of(((s_idx * 32 + t_idx) * ROWS + lane).astype(F32))
    cx = (total[1:2] * 16.0 + total[2:3]) * inv
    cy = total[3:4] * inv
    flow_ref[0:1, :] = (cx - ox) * (1.0 / W_GRID)
    flow_ref[1:2, :] = (cy - oy) * (1.0 / W_GRID)
    matched_ref[...] = (feats * inv).T.astype(BF16)


def per_device(source_feat, target_feat, proj):
    dma = pltpu.SemaphoreType.DMA
    vmem = pl.BlockSpec(memory_space=pltpu.VMEM)
    return pl.pallas_call(
        kernel,
        out_shape=(
            jax.ShapeDtypeStruct((2, ROWS), F32),
            jax.ShapeDtypeStruct((ROWS, C), BF16),
        ),
        in_specs=[vmem] * 3,
        out_specs=[vmem] * 2,
        scratch_shapes=[
            pltpu.VMEM((2, C, STRIP), BF16),
            pltpu.VMEM((GROUP * ROWS, C), BF16),
            pltpu.VMEM((2, STRIP, C), BF16),
            pltpu.VMEM((2, C + AUG, STRIP), BF16),
            pltpu.VMEM((2, STRIP, 2 * ROWS), F32),
            pltpu.VMEM((1, 2 * ROWS), F32),
            pltpu.VMEM((GROUP, C, ROWS), BF16),
            pltpu.VMEM((GROUP, 8, ROWS), F32),
            pltpu.VMEM((GROUP, C, ROWS), BF16),
            pltpu.VMEM((GROUP, 8, ROWS), F32),
            dma((6,)),
            dma((6,)),
            dma((7,)),
            dma((7,)),
            dma((GROUP,)),
            dma((GROUP,)),
            dma((GROUP,)),
            dma((GROUP,)),
            dma((GROUP,)),
            dma((GROUP,)),
        ],
        compiler_params=pltpu.CompilerParams(
            collective_id=0, has_side_effects=True, vmem_limit_bytes=50 << 20
        ),
        name="match_kernel",
    )(source_feat, target_feat.T, proj)


def solution(mesh):
    in_specs = (P(("src", "tgt"), None), P("tgt", "src"), P())
    out_specs = (P(None, ("src", "tgt")), P(("src", "tgt"), None))
    return jax.shard_map(
        per_device, mesh=mesh, in_specs=in_specs, out_specs=out_specs, check_vma=False
    )
```

```python
import jax
import jax.numpy as jnp
from jax import lax
from jax.experimental import pallas as pl
from jax.experimental.pallas import tpu as pltpu
from jax.sharding import PartitionSpec as P

MESH = pl.DeviceIdType.MESH
W_GRID = 320
C = 256
ROWS = 128
STRIP = 1800
CROWS = 64
HCH = CROWS // 2
N = 4
GROUP = N * N
AUG = 16
TOP = 4
F32 = jnp.float32
BF16 = jnp.bfloat16
NT = (((1,), (1,)), ((), ()))
TN = (((0,), (0,)), ((), ()))
RING = ((1, 0, 0), (-1, 0, 1), (1, 0, 1), (-1, 0, 0), (1, -1, 0), (-1, 1, 1))


def place():
    s, t = lax.axis_index("src"), lax.axis_index("tgt")
    return (t // 4 % 2) * 2 + s // 2, t // 8, t % 4, s % 2


def device(x, y, z, c):
    return ((x % 2) * 2 + c, (y * 2 + x // 2) * 4 + z)


def grid_of(pos):
    gy = jnp.floor((pos + 0.5) * (1.0 / W_GRID))
    return pos - gy * W_GRID, gy


def merge(feats, stats):
    top = stats[0][TOP : TOP + 1]
    for stat in stats[1:]:
        top = jnp.maximum(top, stat[TOP : TOP + 1])
    feat_sum = stat_sum = None
    for feat, stat in zip(feats, stats):
        f = jnp.exp(stat[TOP : TOP + 1] - top)
        feat, stat = feat.astype(F32) * f, stat * f
        feat_sum = feat if feat_sum is None else feat_sum + feat
        stat_sum = stat if stat_sum is None else stat_sum + stat
    return top, feat_sum, stat_sum


def kernel(
    src_hbm,
    tgt_hbm,
    proj_hbm,
    flow_ref,
    matched_ref,
    src_ref,
    proj_ref,
    chans,
    qbuf,
    keys,
    keys_t,
    scores,
    top_ref,
    stage,
    sstage,
    inbox,
    sinbox,
    rout,
    srout,
    rin,
    srin,
    in_sems,
    p_send,
    p_recv,
    f_send,
    f_recv,
    q1_send,
    q1_recv,
    q2_send,
    q2_recv,
    o_send,
    o_recv,
    t_send,
    t_recv,
    ro_send,
    ro_recv,
    rt_send,
    rt_recv,
):
    x, y, z, c = place()
    a, b = z + c * (y - z), y + c * (z - y)

    def peer(da, db):
        aa, bb = (a + da) % N, (b + db) % N
        return device(x, bb + c * (aa - bb), aa + c * (bb - aa), c)

    sibling = device(x, y, z, 1 - c)
    left, right = device((x + 3) % N, y, z, c), device((x + 1) % N, y, z, c)

    def piece(dx, cc, start, size):
        xx = (x + dx) % N
        first = ((xx % 2) * 2 + cc) * CROWS + start
        return chans.at[xx // 2, pl.ds(pl.multiple_of(first, HCH), size)]

    loads = (
        pltpu.make_async_copy(tgt_hbm, piece(0, c, 0, CROWS), in_sems.at[0]),
        pltpu.make_async_copy(proj_hbm, proj_ref, in_sems.at[1]),
        pltpu.make_async_copy(src_hbm, src_ref, in_sems.at[2]),
    )
    barrier = pltpu.get_barrier_semaphore()
    for other in (left, right, sibling):
        pl.semaphore_signal(barrier, inc=1, device_id=other, device_id_type=MESH)
    for k in range(1, N):
        pl.semaphore_signal(barrier, inc=1, device_id=peer(k, 0), device_id_type=MESH)
        pl.semaphore_signal(barrier, inc=1, device_id=peer(0, k), device_id_type=MESH)
    for load in loads:
        load.start()
    pl.semaphore_wait(barrier, 3 + 2 * (N - 1))

    def remote(src, dst, send_sem, recv_sem, other):
        return pltpu.make_async_remote_copy(
            src_ref=src,
            dst_ref=dst,
            send_sem=send_sem,
            recv_sem=recv_sem,
            device_id=other,
            device_id_type=MESH,
        )

    def ring_copy(k, arrival):
        step, owner, h = RING[k]
        ref = piece(owner - step * arrival + N, c, h * HCH, HCH)
        fresh = owner == 0 and not arrival
        src = tgt_hbm.at[pl.ds(h * HCH, HCH)] if fresh else ref
        return remote(src, ref, p_send.at[k], p_recv.at[k], right if step == 1 else left)

    def core_copy(k, arrival):
        cc = 1 - c if arrival else c
        if k == len(RING):
            ref = piece(0, cc, 0, CROWS)
        else:
            step, owner, h = RING[k]
            ref = piece(owner - step + N, cc, h * HCH, HCH)
        src = tgt_hbm if k == len(RING) and not arrival else ref
        return remote(src, ref, f_send.at[k], f_recv.at[k], sibling)

    def q_block(k, arrival):
        ref = qbuf.at[b * N + (a + (N - k if arrival else 0)) % N]
        return remote(ref, ref, q1_send.at[k], q1_recv.at[k], peer(k, 0))

    def q_row(k, arrival):
        row = (b + (N - k if arrival else 0)) % N
        ref = qbuf.at[pl.ds(row * N, N)]
        return remote(ref, ref, q2_send.at[k], q2_recv.at[k], peer(0, k))

    def feat_copy(r, j):
        i = r * N + j
        return remote(stage.at[i], inbox.at[i], o_send.at[i], o_recv.at[i], peer(j, 0))

    def stat_copy(r, j):
        i = r * N + j
        return remote(sstage.at[i], sinbox.at[i], t_send.at[i], t_recv.at[i], peer(j, 0))

    def relay_feat(r):
        return remote(rout.at[r], rin.at[r], ro_send.at[r], ro_recv.at[r], peer(0, r))

    def relay_stat(r):
        return remote(srout.at[r], srin.at[r], rt_send.at[r], rt_recv.at[r], peer(0, r))

    for k in range(4):
        ring_copy(k, False).start()
    core_copy(6, False).start()

    for load in loads:
        load.wait()
    queries = jnp.dot(src_ref[...], proj_ref[...], preferred_element_type=F32).astype(BF16)
    qbuf[b * N + a] = (queries.astype(F32) * (1.0 / 16.0)).astype(BF16)
    for k in range(1, N):
        q_block(k, False).start()

    mine = x // 2
    col = lax.broadcasted_iota(jnp.int32, (1, STRIP), 1)
    row = lax.broadcasted_iota(jnp.int32, (AUG, STRIP), 0)
    for e in range(2):
        strip = mine if e == 0 else 1 - mine
        base = ((y * 2 + strip) * 4 + z) * STRIP
        kx, ky = grid_of((base + col).astype(F32))
        kxh = jnp.floor(kx * (1.0 / 16.0))
        kxl = kx - 16.0 * kxh
        aug = jnp.where(
            row == 0,
            1.0,
            jnp.where(row == 1, kxh, jnp.where(row == 2, kxl, jnp.where(row == 3, ky, 0.0))),
        )
        keys_t[e, C : C + AUG, :] = aug.astype(BF16)

    def project(e):
        block = chans[mine if e == 0 else 1 - mine]
        keys[e] = lax.dot_general(block, proj_ref[...], TN, preferred_element_type=F32).astype(BF16)
        keys_t[e, 0:C, :] = lax.dot_general(
            proj_ref[...], block, TN, preferred_element_type=F32
        ).astype(BF16)

    for k in range(2):
        ring_copy(k, True).wait_recv()
        ring_copy(k + 4, False).start()
        core_copy(k, False).start()
    for k in range(1, N):
        q_block(k, True).wait_recv()
    for k in (3, 2, 1):
        q_row(k, False).start()
    for k in range(2, 4):
        ring_copy(k, True).wait_recv()
        core_copy(k, False).start()
    for k in (6, 0, 1, 2, 3):
        core_copy(k, True).wait_recv()
    project(0)
    for k in range(4, 6):
        ring_copy(k, True).wait_recv()
        core_copy(k, False).start()
    for k in range(4, 6):
        core_copy(k, True).wait_recv()
    project(1)

    def relay(r):
        for j in range(1, N):
            feat_copy(r, j).wait_recv()
            stat_copy(r, j).wait_recv()
        i = r * N
        top, feat, stat = merge(
            [stage[i]] + [inbox[i + j] for j in range(1, N)],
            [sstage[i]] + [sinbox[i + j] for j in range(1, N)],
        )
        srow = lax.broadcasted_iota(jnp.int32, (8, ROWS), 0)
        rout[r] = feat.astype(BF16)
        srout[r] = jnp.where(srow == TOP, top, stat)
        relay_feat(r).start()
        relay_stat(r).start()

    def turn(t, carry):
        r = (t // 2 + 1) % N
        js = (2 * (t % 2) + 1, (2 * (t % 2) + 2) % N)

        @pl.when((t % 2 == 0) & (t < 6))
        def _():
            q_row(N - r, True).wait_recv()

        def match(_, inner):
            base = ((b + r) % N) * N
            q = jnp.concatenate([qbuf[base + (a + j) % N] for j in js], axis=0)
            tops = []
            for e in range(2):
                s = lax.dot_general(keys[e], q, NT, preferred_element_type=F32)
                scores[e] = s
                tops.append(jnp.max(s, axis=0, keepdims=True))
            top_ref[...] = jnp.maximum(tops[0], tops[1])
            return inner

        def gather(_, inner):
            m = top_ref[...]
            o = jnp.zeros((C + AUG, 2 * ROWS), F32)
            for e in range(2):
                w = jnp.exp(scores[e] - m).astype(BF16)
                o = o + jnp.dot(keys_t[e], w, preferred_element_type=F32)
            srow = lax.broadcasted_iota(jnp.int32, (8, 2 * ROWS), 0)
            stat = jnp.where(srow == TOP, m, o[C : C + 8, :])
            for e, j in enumerate(js):
                lanes = slice(e * ROWS, (e + 1) * ROWS)
                stage[r * N + j] = o[:C, lanes].astype(BF16)
                sstage[r * N + j] = stat[:, lanes]

                @pl.when(j > 0)
                def _():
                    feat_copy(r, j).start()
                    stat_copy(r, j).start()

            return inner

        lax.fori_loop(t, t + 1, match, 0)
        lax.fori_loop(t, t + 1, gather, 0)

        @pl.when((t % 2 == 1) & (t > 1))
        def _():
            relay((t - 1) // 2)

        return carry

    lax.fori_loop(0, 2 * N, turn, 0)

    for j in range(1, N):
        feat_copy(0, j).wait_recv()
        stat_copy(0, j).wait_recv()
    for r in range(1, N):
        relay_feat(r).wait_recv()
        relay_stat(r).wait_recv()
    _, feats, total = merge(
        [stage[0]] + [inbox[j] for j in range(1, N)] + [rin[r] for r in range(1, N)],
        [sstage[0]] + [sinbox[j] for j in range(1, N)] + [srin[r] for r in range(1, N)],
    )
    inv = 1.0 / total[0:1]
    s_idx, t_idx = lax.axis_index("src"), lax.axis_index("tgt")
    lane = lax.broadcasted_iota(jnp.int32, (1, ROWS), 1)
    ox, oy = grid_of(((s_idx * 32 + t_idx) * ROWS + lane).astype(F32))
    cx = (total[1:2] * 16.0 + total[2:3]) * inv
    cy = total[3:4] * inv
    flow_ref[0:1, :] = (cx - ox) * (1.0 / W_GRID)
    flow_ref[1:2, :] = (cy - oy) * (1.0 / W_GRID)
    matched_ref[...] = (feats * inv).T.astype(BF16)

    for k in range(6):
        ring_copy(k, False).wait_send()
    for k in range(7):
        core_copy(k, False).wait_send()
    for k in range(1, N):
        q_block(k, False).wait_send()
        q_row(k, False).wait_send()
        relay_feat(k).wait_send()
        relay_stat(k).wait_send()

    def settle(i, carry):
        r, j = i // (N - 1), i % (N - 1) + 1
        feat_copy(r, j).wait_send()
        stat_copy(r, j).wait_send()
        return carry

    lax.fori_loop(0, N * (N - 1), settle, 0)


def per_device(source_feat, target_feat, proj):
    dma = pltpu.SemaphoreType.DMA
    vmem = pl.BlockSpec(memory_space=pltpu.VMEM)
    args = (source_feat, target_feat.T, proj)
    return pl.pallas_call(
        kernel,
        out_shape=(
            jax.ShapeDtypeStruct((2, ROWS), F32),
            jax.ShapeDtypeStruct((ROWS, C), BF16),
        ),
        in_specs=[pl.BlockSpec(memory_space=pltpu.HBM)] * 3,
        out_specs=[vmem] * 2,
        scratch_shapes=[
            pltpu.VMEM((ROWS, C), BF16),
            pltpu.VMEM((C, C), BF16),
            pltpu.VMEM((2, C, STRIP), BF16),
            pltpu.VMEM((GROUP, ROWS, C), BF16),
            pltpu.VMEM((2, STRIP, C), BF16),
            pltpu.VMEM((2, C + AUG, STRIP), BF16),
            pltpu.VMEM((2, STRIP, 2 * ROWS), F32),
            pltpu.VMEM((1, 2 * ROWS), F32),
            pltpu.VMEM((GROUP, C, ROWS), BF16),
            pltpu.VMEM((GROUP, 8, ROWS), F32),
            pltpu.VMEM((GROUP, C, ROWS), BF16),
            pltpu.VMEM((GROUP, 8, ROWS), F32),
            pltpu.VMEM((N, C, ROWS), BF16),
            pltpu.VMEM((N, 8, ROWS), F32),
            pltpu.VMEM((N, C, ROWS), BF16),
            pltpu.VMEM((N, 8, ROWS), F32),
            dma((3,)),
            dma((6,)),
            dma((6,)),
            dma((7,)),
            dma((7,)),
            dma((N,)),
            dma((N,)),
            dma((N,)),
            dma((N,)),
            dma((GROUP,)),
            dma((GROUP,)),
            dma((GROUP,)),
            dma((GROUP,)),
            dma((N,)),
            dma((N,)),
            dma((N,)),
            dma((N,)),
        ],
        compiler_params=pltpu.CompilerParams(
            collective_id=0, has_side_effects=True, vmem_limit_bytes=50 << 20
        ),
        name="match_kernel",
    )(*(pltpu.with_memory_space_constraint(arg, pltpu.HBM) for arg in args))


def solution(mesh):
    in_specs = (P(("src", "tgt"), None), P("tgt", "src"), P())
    out_specs = (P(None, ("src", "tgt")), P(("src", "tgt"), None))
    return jax.shard_map(
        per_device, mesh=mesh, in_specs=in_specs, out_specs=out_specs, check_vma=False
    )
```

```python
import jax
import jax.numpy as jnp
from jax import lax
from jax.experimental import pallas as pl
from jax.experimental.pallas import tpu as pltpu
from jax.sharding import PartitionSpec as P

MESH = pl.DeviceIdType.MESH
W_GRID = 320
C = 256
ROWS = 128
STRIP = 1800
CROWS = 64
HCH = CROWS // 2
N = 4
GROUP = N * N
AUG = 16
TOP = 4
F32 = jnp.float32
BF16 = jnp.bfloat16
NT = (((1,), (1,)), ((), ()))
TN = (((0,), (0,)), ((), ()))
RING = ((1, 0, 0), (-1, 0, 1), (1, 0, 1), (-1, 0, 0), (1, -1, 0), (-1, 1, 1))


ORDER = (
    (2, 0), (1, 0), (2, 2), (2, 1), (2, 3), (1, 2), (3, 2), (1, 1),
    (1, 3), (3, 1), (3, 3), (0, 2), (3, 0), (0, 1), (0, 3), (0, 0),
)


def table(which, half):
    return sum(ORDER[8 * half + k][which] * 4**k for k in range(8))


def offset(which, i):
    if isinstance(i, int):
        return jnp.int32(ORDER[i][which])
    tab = jnp.where(i < 8, table(which, 0), table(which, 1))
    return lax.shift_right_logical(tab, 2 * (i % 8)) % 4


def place():
    s, t = lax.axis_index("src"), lax.axis_index("tgt")
    return (t // 4 % 2) * 2 + s // 2, t // 8, t % 4, s % 2


def device(x, y, z, c):
    return ((x % 2) * 2 + c, (y * 2 + x // 2) * 4 + z)


def grid_of(pos):
    gy = jnp.floor((pos + 0.5) * (1.0 / W_GRID))
    return pos - gy * W_GRID, gy


def merge(feats, stats):
    top = stats[0][TOP : TOP + 1]
    for stat in stats[1:]:
        top = jnp.maximum(top, stat[TOP : TOP + 1])
    feat_sum = stat_sum = None
    for feat, stat in zip(feats, stats):
        f = jnp.exp(stat[TOP : TOP + 1] - top)
        feat, stat = feat.astype(F32) * f, stat * f
        feat_sum = feat if feat_sum is None else feat_sum + feat
        stat_sum = stat if stat_sum is None else stat_sum + stat
    return top, feat_sum, stat_sum


def kernel(
    src_hbm,
    tgt_hbm,
    proj_hbm,
    flow_ref,
    matched_ref,
    src_ref,
    proj_ref,
    chans,
    qbuf,
    keys,
    keys_t,
    scores_a,
    scores_b,
    top_ref,
    stage,
    sstage,
    inbox,
    sinbox,
    rout,
    srout,
    rin,
    srin,
    in_sems,
    p_send,
    p_recv,
    f_send,
    f_recv,
    q1_send,
    q1_recv,
    q2_send,
    q2_recv,
    o_send,
    o_recv,
    t_send,
    t_recv,
    ro_send,
    ro_recv,
    rt_send,
    rt_recv,
):
    x, y, z, c = place()
    a, b = z + c * (y - z), y + c * (z - y)

    def peer(da, db):
        aa, bb = (a + da) % N, (b + db) % N
        return device(x, bb + c * (aa - bb), aa + c * (bb - aa), c)

    sibling = device(x, y, z, 1 - c)
    left, right = device((x + 3) % N, y, z, c), device((x + 1) % N, y, z, c)

    def piece(dx, cc, start, size):
        xx = (x + dx) % N
        first = ((xx % 2) * 2 + cc) * CROWS + start
        return chans.at[xx // 2, pl.ds(pl.multiple_of(first, HCH), size)]

    loads = (
        pltpu.make_async_copy(tgt_hbm, piece(0, c, 0, CROWS), in_sems.at[0]),
        pltpu.make_async_copy(proj_hbm, proj_ref, in_sems.at[1]),
        pltpu.make_async_copy(src_hbm, src_ref, in_sems.at[2]),
    )
    for load in loads:
        load.start()
    barrier = pltpu.get_barrier_semaphore()
    others = [(k, 0) for k in range(1, N)] + [(0, k) for k in range(1, N)]
    for other in (left, right, sibling):
        pl.semaphore_signal(barrier, inc=1, device_id=other, device_id_type=MESH)
    for da, db in others:
        pl.semaphore_signal(barrier, inc=1, device_id=peer(da, db), device_id_type=MESH)
    for load in loads:
        load.wait()
    queries = jnp.dot(src_ref[...], proj_ref[...], preferred_element_type=F32).astype(BF16)
    qbuf[b * N + a] = (queries.astype(F32) * (1.0 / 16.0)).astype(BF16)
    pl.semaphore_wait(barrier, 3 + len(others))

    def remote(src, dst, send_sem, recv_sem, other):
        return pltpu.make_async_remote_copy(
            src_ref=src,
            dst_ref=dst,
            send_sem=send_sem,
            recv_sem=recv_sem,
            device_id=other,
            device_id_type=MESH,
        )

    def ring_copy(k, arrival):
        step, owner, h = RING[k]
        ref = piece(owner - step * arrival + N, c, h * HCH, HCH)
        fresh = owner == 0 and not arrival
        src = tgt_hbm.at[pl.ds(h * HCH, HCH)] if fresh else ref
        return remote(src, ref, p_send.at[k], p_recv.at[k], right if step == 1 else left)

    def core_copy(k, arrival):
        cc = 1 - c if arrival else c
        if k == len(RING):
            ref = piece(0, cc, 0, CROWS)
        else:
            step, owner, h = RING[k]
            ref = piece(owner - step + N, cc, h * HCH, HCH)
        src = tgt_hbm if k == len(RING) and not arrival else ref
        return remote(src, ref, f_send.at[k], f_recv.at[k], sibling)

    def q_block(k, arrival):
        ref = qbuf.at[b * N + (a + (N - k if arrival else 0)) % N]
        return remote(ref, ref, q1_send.at[k], q1_recv.at[k], peer(k, 0))

    def q_cross(v, k, arrival):
        row = (b + (N - v if arrival else 0)) % N
        ref = qbuf.at[row * N + (a + N - k) % N]
        i = v * N + k
        return remote(ref, ref, q2_send.at[i], q2_recv.at[i], peer(0, v))

    def feat_copy(r, j):
        i = r * N + j
        return remote(stage.at[i], inbox.at[i], o_send.at[i], o_recv.at[i], peer(j, 0))

    def stat_copy(r, j):
        i = r * N + j
        return remote(sstage.at[i], sinbox.at[i], t_send.at[i], t_recv.at[i], peer(j, 0))

    def relay_feat(r):
        return remote(rout.at[r], rin.at[r], ro_send.at[r], ro_recv.at[r], peer(0, r))

    def relay_stat(r):
        return remote(srout.at[r], srin.at[r], rt_send.at[r], rt_recv.at[r], peer(0, r))

    for k in range(4):
        ring_copy(k, False).start()
    core_copy(6, False).start()

    for k in (1, 3, 2):
        q_block(k, False).start()

    def pass_on(k):
        for v in (2, 1, 3):
            q_cross(v, k, False).start()

    pass_on(0)

    mine = x // 2
    col = lax.broadcasted_iota(jnp.int32, (1, STRIP), 1)
    row = lax.broadcasted_iota(jnp.int32, (AUG, STRIP), 0)
    for e in range(2):
        strip = mine if e == 0 else 1 - mine
        base = ((y * 2 + strip) * 4 + z) * STRIP
        kx, ky = grid_of((base + col).astype(F32))
        kxh = jnp.floor(kx * (1.0 / 16.0))
        kxl = kx - 16.0 * kxh
        aug = jnp.where(
            row == 0,
            1.0,
            jnp.where(row == 1, kxh, jnp.where(row == 2, kxl, jnp.where(row == 3, ky, 0.0))),
        )
        keys_t[e, C : C + AUG, :] = aug.astype(BF16)

    def project(e):
        block = chans[mine if e == 0 else 1 - mine]
        keys[e] = lax.dot_general(block, proj_ref[...], TN, preferred_element_type=F32).astype(BF16)
        keys_t[e, 0:C, :] = lax.dot_general(
            proj_ref[...], block, TN, preferred_element_type=F32
        ).astype(BF16)

    for k in (1, 3):
        q_block(k, True).wait_recv()
        pass_on(k)
    for k in range(2):
        ring_copy(k, True).wait_recv()
        ring_copy(k + 4, False).start()
        core_copy(k, False).start()
    q_block(2, True).wait_recv()
    pass_on(2)
    for k in range(2, 4):
        ring_copy(k, True).wait_recv()
        core_copy(k, False).start()
    for k in (6, 0, 1, 2, 3):
        core_copy(k, True).wait_recv()
    project(0)
    for k in range(4, 6):
        ring_copy(k, True).wait_recv()
        core_copy(k, False).start()

    def relay(r):
        for j in range(1, N):
            feat_copy(r, j).wait_recv()
            stat_copy(r, j).wait_recv()
        i = r * N
        top, feat, stat = merge(
            [stage[i]] + [inbox[i + j] for j in range(1, N)],
            [sstage[i]] + [sinbox[i + j] for j in range(1, N)],
        )
        srow = lax.broadcasted_iota(jnp.int32, (8, ROWS), 0)
        rout[r] = feat.astype(BF16)
        srout[r] = jnp.where(srow == TOP, top, stat)
        relay_feat(r).start()
        relay_stat(r).start()

    def apart(body):
        def once(_, carry):
            body()
            return carry

        lax.fori_loop(b, b + 1, once, 0)

    def block(t, e):
        i = 2 * t + e
        return offset(0, i), offset(1, i)

    def await_queries(t):
        for e in range(2):
            r, j = block(t, e)

            @pl.when(r > 0)
            def _():
                q_cross(N - r, (N - j) % N, True).wait_recv()

    def query_pair(t):
        pair = []
        for e in range(2):
            r, j = block(t, e)
            pair.append(qbuf[((b + r) % N) * N + (a + j) % N])
        return jnp.concatenate(pair, axis=0)

    def emit(t, o, m):
        srow = lax.broadcasted_iota(jnp.int32, (8, 2 * ROWS), 0)
        stat = jnp.where(srow == TOP, m, o[C : C + 8, :])
        for e in range(2):
            r, j = block(t, e)
            lanes = slice(e * ROWS, (e + 1) * ROWS)
            stage[r * N + j] = o[:C, lanes].astype(BF16)
            sstage[r * N + j] = stat[:, lanes]

            @pl.when(j > 0)
            def _():
                feat_copy(r, j).start()
                stat_copy(r, j).start()

    def step(t, slot, matching, gathering):
        def body():
            if matching:
                q = query_pair(t + 1)
            if gathering:
                m = top_ref[slot]
            tops, parts = [], []
            for e in range(2):
                if matching:
                    s = lax.dot_general(keys[e], q, NT, preferred_element_type=F32)
                    (scores_b, scores_a)[slot][e] = s
                    tops.append(jnp.max(s, axis=0, keepdims=True))
                if gathering:
                    w = jnp.exp((scores_a, scores_b)[slot][e] - m).astype(BF16)
                    parts.append(jnp.dot(keys_t[e], w, preferred_element_type=F32))
            if matching:
                top_ref[1 - slot] = jnp.maximum(tops[0], tops[1])
            if gathering:
                emit(t, parts[0] + parts[1], m)

        apart(body)

    def first_match(e):
        def body():
            s = lax.dot_general(keys[e], query_pair(0), NT, preferred_element_type=F32)
            scores_a[e] = s
            top = jnp.max(s, axis=0, keepdims=True)
            top_ref[0] = top if e == 0 else jnp.maximum(top_ref[0], top)

        apart(body)

    def two_turns(u, carry):
        await_queries(2 * u + 1)
        step(2 * u, 0, True, True)

        await_queries(2 * u + 2)
        step(2 * u + 1, 1, True, True)
        return carry

    await_queries(0)
    first_match(0)
    for k in range(4, 6):
        core_copy(k, True).wait_recv()
    project(1)
    first_match(1)
    lax.fori_loop(0, N - 1, two_turns, 0)
    relay(2)
    await_queries(2 * N - 1)
    step(2 * N - 2, 0, True, True)
    step(2 * N - 1, 1, False, True)
    relay(1)
    relay(3)

    def await_block(r, j):
        feat_copy(r, j).wait_recv()
        stat_copy(r, j).wait_recv()

    def await_relay(r):
        relay_feat(r).wait_recv()
        relay_stat(r).wait_recv()

    for j in (2, 1):
        await_block(0, j)
    await_relay(2)
    top, feats, total = merge(
        [stage[0], inbox[2], inbox[1], rin[2]],
        [sstage[0], sinbox[2], sinbox[1], srin[2]],
    )
    trow = lax.broadcasted_iota(jnp.int32, (8, ROWS), 0)
    await_block(0, 3)
    for r in (1, 3):
        await_relay(r)
    _, feats, total = merge(
        [feats, inbox[3], rin[1], rin[3]],
        [jnp.where(trow == TOP, top, total), sinbox[3], srin[1], srin[3]],
    )
    inv = 1.0 / total[0:1]
    s_idx, t_idx = lax.axis_index("src"), lax.axis_index("tgt")
    lane = lax.broadcasted_iota(jnp.int32, (1, ROWS), 1)
    ox, oy = grid_of(((s_idx * 32 + t_idx) * ROWS + lane).astype(F32))
    cx = (total[1:2] * 16.0 + total[2:3]) * inv
    cy = total[3:4] * inv
    flow_ref[0:1, :] = (cx - ox) * (1.0 / W_GRID)
    flow_ref[1:2, :] = (cy - oy) * (1.0 / W_GRID)
    matched_ref[...] = (feats * inv).T.astype(BF16)

    for k in range(6):
        ring_copy(k, False).wait_send()
    for k in range(7):
        core_copy(k, False).wait_send()
    for k in range(1, N):
        q_block(k, False).wait_send()
    for r in range(1, N):
        relay_feat(r).wait_send()
        relay_stat(r).wait_send()

    def settle(i, carry):
        r, j = i // N, i % N

        @pl.when(r > 0)
        def _():
            q_cross(r, j, False).wait_send()

        @pl.when(j > 0)
        def _():
            feat_copy(r, j).wait_send()
            stat_copy(r, j).wait_send()

        return carry

    lax.fori_loop(0, GROUP, settle, 0)


def per_device(source_feat, target_feat, proj):
    dma = pltpu.SemaphoreType.DMA
    vmem = pl.BlockSpec(memory_space=pltpu.VMEM)
    args = (source_feat, target_feat.T, proj)
    return pl.pallas_call(
        kernel,
        out_shape=(
            jax.ShapeDtypeStruct((2, ROWS), F32),
            jax.ShapeDtypeStruct((ROWS, C), BF16),
        ),
        in_specs=[pl.BlockSpec(memory_space=pltpu.HBM)] * 3,
        out_specs=[vmem] * 2,
        scratch_shapes=[
            pltpu.VMEM((ROWS, C), BF16),
            pltpu.VMEM((C, C), BF16),
            pltpu.VMEM((2, C, STRIP), BF16),
            pltpu.VMEM((GROUP, ROWS, C), BF16),
            pltpu.VMEM((2, STRIP, C), BF16),
            pltpu.VMEM((2, C + AUG, STRIP), BF16),
            pltpu.VMEM((2, STRIP, 2 * ROWS), F32),
            pltpu.VMEM((2, STRIP, 2 * ROWS), F32),
            pltpu.VMEM((2, 1, 2 * ROWS), F32),
            pltpu.VMEM((GROUP, C, ROWS), BF16),
            pltpu.VMEM((GROUP, 8, ROWS), F32),
            pltpu.VMEM((GROUP, C, ROWS), BF16),
            pltpu.VMEM((GROUP, 8, ROWS), F32),
            pltpu.VMEM((N, C, ROWS), BF16),
            pltpu.VMEM((N, 8, ROWS), F32),
            pltpu.VMEM((N, C, ROWS), BF16),
            pltpu.VMEM((N, 8, ROWS), F32),
            dma((3,)),
            dma((6,)),
            dma((6,)),
            dma((7,)),
            dma((7,)),
            dma((N,)),
            dma((N,)),
            dma((GROUP,)),
            dma((GROUP,)),
            dma((GROUP,)),
            dma((GROUP,)),
            dma((GROUP,)),
            dma((GROUP,)),
            dma((N,)),
            dma((N,)),
            dma((N,)),
            dma((N,)),
        ],
        compiler_params=pltpu.CompilerParams(
            collective_id=0, has_side_effects=True, vmem_limit_bytes=50 << 20
        ),
        name="match_kernel",
    )(*(pltpu.with_memory_space_constraint(arg, pltpu.HBM) for arg in args))


def solution(mesh):
    in_specs = (P(("src", "tgt"), None), P("tgt", "src"), P())
    out_specs = (P(None, ("src", "tgt")), P(("src", "tgt"), None))
    return jax.shard_map(
        per_device, mesh=mesh, in_specs=in_specs, out_specs=out_specs, check_vma=False
    )
```

```python
import jax
import jax.numpy as jnp
from jax import lax
from jax.experimental import pallas as pl
from jax.experimental.pallas import tpu as pltpu
from jax.sharding import PartitionSpec as P

MESH = pl.DeviceIdType.MESH
W_GRID = 320
C = 256
ROWS = 128
STRIP = 1800
CROWS = 64
HCH = CROWS // 2
N = 4
GROUP = N * N
PACKED = C + 32
AUG = 16
TOP = 4
F32 = jnp.float32
BF16 = jnp.bfloat16
NT = (((1,), (1,)), ((), ()))
TN = (((0,), (0,)), ((), ()))
RING = ((1, 0, 0), (-1, 0, 1), (1, 0, 1), (-1, 0, 0), (1, -1, 0), (-1, 1, 1))


ORDER = (
    (2, 0), (1, 0), (2, 2), (2, 1), (2, 3), (1, 2), (3, 2), (1, 1),
    (1, 3), (3, 1), (3, 3), (0, 2), (3, 0), (0, 1), (0, 3), (0, 0),
)


def table(which, half):
    return sum(ORDER[8 * half + k][which] * 4**k for k in range(8))


def offset(which, i):
    if isinstance(i, int):
        return jnp.int32(ORDER[i][which])
    tab = jnp.where(i < 8, table(which, 0), table(which, 1))
    return lax.shift_right_logical(tab, 2 * (i % 8)) % 4


def place():
    s, t = lax.axis_index("src"), lax.axis_index("tgt")
    return (t // 4 % 2) * 2 + s // 2, t // 8, t % 4, s % 2


def device(x, y, z, c):
    return ((x % 2) * 2 + c, (y * 2 + x // 2) * 4 + z)


def grid_of(pos):
    gy = jnp.floor((pos + 0.5) * (1.0 / W_GRID))
    return pos - gy * W_GRID, gy


def spread(stat):
    high = stat.astype(BF16).astype(F32)
    middle = (stat - high).astype(BF16).astype(F32)
    parts = [high, middle, stat - high - middle, jnp.zeros_like(stat)]
    return jnp.concatenate(parts, axis=0).astype(BF16)


def whole(block):
    parts = block[C:].astype(F32)
    return block[:C], parts[0:8] + parts[8:16] + parts[16:24]


def merge(blocks):
    feats, stats = zip(*blocks)
    top = stats[0][TOP : TOP + 1]
    for stat in stats[1:]:
        top = jnp.maximum(top, stat[TOP : TOP + 1])
    feat_sum = stat_sum = None
    for feat, stat in zip(feats, stats):
        f = jnp.exp(stat[TOP : TOP + 1] - top)
        feat, stat = feat.astype(F32) * f, stat * f
        feat_sum = feat if feat_sum is None else feat_sum + feat
        stat_sum = stat if stat_sum is None else stat_sum + stat
    return top, feat_sum, stat_sum


def kernel(
    src_hbm,
    tgt_hbm,
    proj_hbm,
    flow_ref,
    matched_ref,
    src_ref,
    proj_ref,
    chans,
    qbuf,
    keys,
    keys_t,
    scores_a,
    scores_b,
    top_ref,
    stage,
    inbox,
    rout,
    rin,
    in_sems,
    p_send,
    p_recv,
    f_send,
    f_recv,
    q1_send,
    q1_recv,
    q2_send,
    q2_recv,
    o_send,
    o_recv,
    ro_send,
    ro_recv,
):
    x, y, z, c = place()
    a, b = z + c * (y - z), y + c * (z - y)

    def peer(da, db):
        aa, bb = (a + da) % N, (b + db) % N
        return device(x, bb + c * (aa - bb), aa + c * (bb - aa), c)

    sibling = device(x, y, z, 1 - c)
    left, right = device((x + 3) % N, y, z, c), device((x + 1) % N, y, z, c)

    def piece(dx, cc, start, size):
        xx = (x + dx) % N
        first = ((xx % 2) * 2 + cc) * CROWS + start
        return chans.at[xx // 2, pl.ds(pl.multiple_of(first, HCH), size)]

    loads = (
        pltpu.make_async_copy(tgt_hbm, piece(0, c, 0, CROWS), in_sems.at[0]),
        pltpu.make_async_copy(proj_hbm, proj_ref, in_sems.at[1]),
        pltpu.make_async_copy(src_hbm, src_ref, in_sems.at[2]),
    )
    for load in loads:
        load.start()
    barrier = pltpu.get_barrier_semaphore()
    others = [(k, 0) for k in range(1, N)] + [(0, k) for k in range(1, N)]
    for other in (left, right, sibling):
        pl.semaphore_signal(barrier, inc=1, device_id=other, device_id_type=MESH)
    for da, db in others:
        pl.semaphore_signal(barrier, inc=1, device_id=peer(da, db), device_id_type=MESH)
    pl.semaphore_wait(barrier, 3 + len(others))

    def remote(src, dst, send_sem, recv_sem, other):
        return pltpu.make_async_remote_copy(
            src_ref=src,
            dst_ref=dst,
            send_sem=send_sem,
            recv_sem=recv_sem,
            device_id=other,
            device_id_type=MESH,
        )

    def ring_copy(k, arrival):
        step, owner, h = RING[k]
        ref = piece(owner - step * arrival + N, c, h * HCH, HCH)
        fresh = owner == 0 and not arrival
        src = tgt_hbm.at[pl.ds(h * HCH, HCH)] if fresh else ref
        return remote(src, ref, p_send.at[k], p_recv.at[k], right if step == 1 else left)

    def core_copy(k, arrival):
        cc = 1 - c if arrival else c
        if k == len(RING):
            ref = piece(0, cc, 0, CROWS)
        else:
            step, owner, h = RING[k]
            ref = piece(owner - step + N, cc, h * HCH, HCH)
        src = tgt_hbm if k == len(RING) and not arrival else ref
        return remote(src, ref, f_send.at[k], f_recv.at[k], sibling)

    def q_block(k, arrival):
        ref = qbuf.at[b * N + (a + (N - k if arrival else 0)) % N]
        return remote(ref, ref, q1_send.at[k], q1_recv.at[k], peer(k, 0))

    def q_cross(v, k, arrival):
        row = (b + (N - v if arrival else 0)) % N
        ref = qbuf.at[row * N + (a + N - k) % N]
        i = v * N + k
        return remote(ref, ref, q2_send.at[i], q2_recv.at[i], peer(0, v))

    def feat_copy(r, j):
        i = r * N + j
        return remote(stage.at[i], inbox.at[i], o_send.at[i], o_recv.at[i], peer(j, 0))

    def relay_feat(r):
        return remote(rout.at[r], rin.at[r], ro_send.at[r], ro_recv.at[r], peer(0, r))

    for k in range(4):
        ring_copy(k, False).start()
    core_copy(6, False).start()

    for load in loads:
        load.wait()
    queries = jnp.dot(src_ref[...], proj_ref[...], preferred_element_type=F32).astype(BF16)
    qbuf[b * N + a] = (queries.astype(F32) * (1.0 / 16.0)).astype(BF16)
    for k in (1, 3, 2):
        q_block(k, False).start()

    def pass_on(k):
        for v in (2, 1, 3):
            q_cross(v, k, False).start()

    pass_on(0)

    mine = x // 2
    col = lax.broadcasted_iota(jnp.int32, (1, STRIP), 1)
    row = lax.broadcasted_iota(jnp.int32, (AUG, STRIP), 0)
    for e in range(2):
        strip = mine if e == 0 else 1 - mine
        base = ((y * 2 + strip) * 4 + z) * STRIP
        kx, ky = grid_of((base + col).astype(F32))
        kxh = jnp.floor(kx * (1.0 / 16.0))
        kxl = kx - 16.0 * kxh
        aug = jnp.where(
            row == 0,
            1.0,
            jnp.where(row == 1, kxh, jnp.where(row == 2, kxl, jnp.where(row == 3, ky, 0.0))),
        )
        keys_t[e, C : C + AUG, :] = aug.astype(BF16)

    def project(e):
        block = chans[mine if e == 0 else 1 - mine]
        keys[e] = lax.dot_general(block, proj_ref[...], TN, preferred_element_type=F32).astype(BF16)
        keys_t[e, 0:C, :] = lax.dot_general(
            proj_ref[...], block, TN, preferred_element_type=F32
        ).astype(BF16)

    for k in (1, 3):
        q_block(k, True).wait_recv()
        pass_on(k)
    for k in range(2):
        ring_copy(k, True).wait_recv()
        ring_copy(k + 4, False).start()
        core_copy(k, False).start()
    q_block(2, True).wait_recv()
    pass_on(2)
    for k in range(2, 4):
        ring_copy(k, True).wait_recv()
        core_copy(k, False).start()
    for k in (6, 0, 1, 2, 3):
        core_copy(k, True).wait_recv()
    project(0)
    for k in range(4, 6):
        ring_copy(k, True).wait_recv()
        core_copy(k, False).start()

    def relay(r):
        for j in range(1, N):
            feat_copy(r, j).wait_recv()
        i = r * N
        top, feat, stat = merge(
            [whole(stage[i])] + [whole(inbox[i + j]) for j in range(1, N)]
        )
        srow = lax.broadcasted_iota(jnp.int32, (8, ROWS), 0)
        rout[r, 0:C] = feat.astype(BF16)
        rout[r, C:PACKED] = spread(jnp.where(srow == TOP, top, stat))
        relay_feat(r).start()

    def apart(body):
        def once(_, carry):
            body()
            return carry

        lax.fori_loop(b, b + 1, once, 0)

    def block(t, e):
        i = 2 * t + e
        return offset(0, i), offset(1, i)

    def await_queries(t):
        for e in range(2):
            r, j = block(t, e)

            @pl.when(r > 0)
            def _():
                q_cross(N - r, (N - j) % N, True).wait_recv()

    def query_pair(t):
        pair = []
        for e in range(2):
            r, j = block(t, e)
            pair.append(qbuf[((b + r) % N) * N + (a + j) % N])
        return jnp.concatenate(pair, axis=0)

    def emit(t, o, m):
        srow = lax.broadcasted_iota(jnp.int32, (8, 2 * ROWS), 0)
        stat = spread(jnp.where(srow == TOP, m, o[C : C + 8, :]))
        for e in range(2):
            r, j = block(t, e)
            lanes = slice(e * ROWS, (e + 1) * ROWS)
            stage[r * N + j, 0:C] = o[:C, lanes].astype(BF16)
            stage[r * N + j, C:PACKED] = stat[:, lanes]

            @pl.when(j > 0)
            def _():
                feat_copy(r, j).start()

    def step(t, slot, matching, gathering):
        def body():
            if matching:
                q = query_pair(t + 1)
            if gathering:
                m = top_ref[slot]
            tops, parts = [], []
            for e in range(2):
                if matching:
                    s = lax.dot_general(keys[e], q, NT, preferred_element_type=F32)
                    (scores_b, scores_a)[slot][e] = s
                    tops.append(jnp.max(s, axis=0, keepdims=True))
                if gathering:
                    w = jnp.exp((scores_a, scores_b)[slot][e] - m).astype(BF16)
                    parts.append(jnp.dot(keys_t[e], w, preferred_element_type=F32))
            if matching:
                top_ref[1 - slot] = jnp.maximum(tops[0], tops[1])
            if gathering:
                emit(t, parts[0] + parts[1], m)

        apart(body)

    def first_match(e):
        def body():
            s = lax.dot_general(keys[e], query_pair(0), NT, preferred_element_type=F32)
            scores_a[e] = s
            top = jnp.max(s, axis=0, keepdims=True)
            top_ref[0] = top if e == 0 else jnp.maximum(top_ref[0], top)

        apart(body)

    def two_turns(u, carry):
        await_queries(2 * u + 1)
        step(2 * u, 0, True, True)

        await_queries(2 * u + 2)
        step(2 * u + 1, 1, True, True)
        return carry

    await_queries(0)
    first_match(0)
    for k in range(4, 6):
        core_copy(k, True).wait_recv()
    project(1)
    first_match(1)
    lax.fori_loop(0, N - 1, two_turns, 0)
    relay(2)
    await_queries(2 * N - 1)
    step(2 * N - 2, 0, True, True)
    step(2 * N - 1, 1, False, True)
    relay(1)
    relay(3)

    def await_block(r, j):
        feat_copy(r, j).wait_recv()

    def await_relay(r):
        relay_feat(r).wait_recv()

    for j in (2, 1):
        await_block(0, j)
    await_relay(2)
    top, feats, total = merge(
        [whole(stage[0]), whole(inbox[2]), whole(inbox[1]), whole(rin[2])]
    )
    trow = lax.broadcasted_iota(jnp.int32, (8, ROWS), 0)
    await_block(0, 3)
    for r in (1, 3):
        await_relay(r)
    _, feats, total = merge(
        [(feats, jnp.where(trow == TOP, top, total))]
        + [whole(block) for block in (inbox[3], rin[1], rin[3])]
    )
    inv = 1.0 / total[0:1]
    s_idx, t_idx = lax.axis_index("src"), lax.axis_index("tgt")
    lane = lax.broadcasted_iota(jnp.int32, (1, ROWS), 1)
    ox, oy = grid_of(((s_idx * 32 + t_idx) * ROWS + lane).astype(F32))
    cx = (total[1:2] * 16.0 + total[2:3]) * inv
    cy = total[3:4] * inv
    flow_ref[0:1, :] = (cx - ox) * (1.0 / W_GRID)
    flow_ref[1:2, :] = (cy - oy) * (1.0 / W_GRID)
    matched_ref[...] = (feats * inv).T.astype(BF16)

    for k in range(6):
        ring_copy(k, False).wait_send()
    for k in range(7):
        core_copy(k, False).wait_send()
    for k in range(1, N):
        q_block(k, False).wait_send()
    for r in range(1, N):
        relay_feat(r).wait_send()

    def settle(i, carry):
        r, j = i // N, i % N

        @pl.when(r > 0)
        def _():
            q_cross(r, j, False).wait_send()

        @pl.when(j > 0)
        def _():
            feat_copy(r, j).wait_send()

        return carry

    lax.fori_loop(0, GROUP, settle, 0)


def per_device(source_feat, target_feat, proj):
    dma = pltpu.SemaphoreType.DMA
    vmem = pl.BlockSpec(memory_space=pltpu.VMEM)
    args = (source_feat, target_feat.T, proj)
    return pl.pallas_call(
        kernel,
        out_shape=(
            jax.ShapeDtypeStruct((2, ROWS), F32),
            jax.ShapeDtypeStruct((ROWS, C), BF16),
        ),
        in_specs=[pl.BlockSpec(memory_space=pltpu.HBM)] * 3,
        out_specs=[vmem] * 2,
        scratch_shapes=[
            pltpu.VMEM((ROWS, C), BF16),
            pltpu.VMEM((C, C), BF16),
            pltpu.VMEM((2, C, STRIP), BF16),
            pltpu.VMEM((GROUP, ROWS, C), BF16),
            pltpu.VMEM((2, STRIP, C), BF16),
            pltpu.VMEM((2, C + AUG, STRIP), BF16),
            pltpu.VMEM((2, STRIP, 2 * ROWS), F32),
            pltpu.VMEM((2, STRIP, 2 * ROWS), F32),
            pltpu.VMEM((2, 1, 2 * ROWS), F32),
            pltpu.VMEM((GROUP, PACKED, ROWS), BF16),
            pltpu.VMEM((GROUP, PACKED, ROWS), BF16),
            pltpu.VMEM((N, PACKED, ROWS), BF16),
            pltpu.VMEM((N, PACKED, ROWS), BF16),
            dma((3,)),
            dma((6,)),
            dma((6,)),
            dma((7,)),
            dma((7,)),
            dma((N,)),
            dma((N,)),
            dma((GROUP,)),
            dma((GROUP,)),
            dma((GROUP,)),
            dma((GROUP,)),
            dma((N,)),
            dma((N,)),
        ],
        compiler_params=pltpu.CompilerParams(
            collective_id=0, has_side_effects=True, vmem_limit_bytes=50 << 20
        ),
        name="match_kernel",
    )(*(pltpu.with_memory_space_constraint(arg, pltpu.HBM) for arg in args))


def solution(mesh):
    in_specs = (P(("src", "tgt"), None), P("tgt", "src"), P())
    out_specs = (P(None, ("src", "tgt")), P(("src", "tgt"), None))
    return jax.shard_map(
        per_device, mesh=mesh, in_specs=in_specs, out_specs=out_specs, check_vma=False
    )
```

```python
import jax
import jax.numpy as jnp
from jax import lax
from jax.experimental import pallas as pl
from jax.experimental.pallas import tpu as pltpu
from jax.sharding import PartitionSpec as P

MESH = pl.DeviceIdType.MESH
W_GRID = 320
C = 256
ROWS = 128
STRIP = 1800
CROWS = 64
HCH = CROWS // 2
N = 4
GROUP = N * N
PACKED = C + 32
AUG = 16
TOP = 4
F32 = jnp.float32
BF16 = jnp.bfloat16
NT = (((1,), (1,)), ((), ()))
TN = (((0,), (0,)), ((), ()))
RING = ((1, 0, 0), (-1, 0, 1), (1, 0, 1), (-1, 0, 0), (1, -1, 0), (-1, 1, 1))


ORDER = (
    (2, 0), (1, 0), (2, 2), (2, 1), (2, 3), (1, 2), (3, 2), (1, 1),
    (1, 3), (3, 1), (3, 3), (0, 2), (3, 0), (0, 1), (0, 3), (0, 0),
)


def table(which, half):
    return sum(ORDER[8 * half + k][which] * 4**k for k in range(8))


def offset(which, i):
    if isinstance(i, int):
        return jnp.int32(ORDER[i][which])
    tab = jnp.where(i < 8, table(which, 0), table(which, 1))
    return lax.shift_right_logical(tab, 2 * (i % 8)) % 4


def place():
    s, t = lax.axis_index("src"), lax.axis_index("tgt")
    return (t // 4 % 2) * 2 + s // 2, t // 8, t % 4, s % 2


def device(x, y, z, c):
    return ((x % 2) * 2 + c, (y * 2 + x // 2) * 4 + z)


def grid_of(pos):
    gy = jnp.floor((pos + 0.5) * (1.0 / W_GRID))
    return pos - gy * W_GRID, gy


def spread(stat):
    high = stat.astype(BF16).astype(F32)
    middle = (stat - high).astype(BF16).astype(F32)
    parts = [high, middle, stat - high - middle, jnp.zeros_like(stat)]
    return jnp.concatenate(parts, axis=0).astype(BF16)


def whole(block):
    parts = block[C:].astype(F32)
    return block[:C], parts[0:8] + parts[8:16] + parts[16:24]


def merge(blocks):
    feats, stats = zip(*blocks)
    top = stats[0][TOP : TOP + 1]
    for stat in stats[1:]:
        top = jnp.maximum(top, stat[TOP : TOP + 1])
    feat_sum = stat_sum = None
    for feat, stat in zip(feats, stats):
        f = jnp.exp(stat[TOP : TOP + 1] - top)
        feat, stat = feat.astype(F32) * f, stat * f
        feat_sum = feat if feat_sum is None else feat_sum + feat
        stat_sum = stat if stat_sum is None else stat_sum + stat
    return top, feat_sum, stat_sum


def kernel(
    src_hbm,
    tgt_hbm,
    proj_hbm,
    flow_ref,
    matched_ref,
    src_ref,
    proj_ref,
    chans,
    qbuf,
    keys,
    keys_t,
    scores_a,
    scores_b,
    top_ref,
    stage,
    inbox,
    rout,
    rin,
    in_sems,
    p_send,
    p_recv,
    f_send,
    f_recv,
    q1_send,
    q1_recv,
    q2_send,
    q2_recv,
    o_send,
    o_recv,
    ro_send,
    ro_recv,
):
    x, y, z, c = place()
    a, b = z + c * (y - z), y + c * (z - y)

    def peer(da, db):
        aa, bb = (a + da) % N, (b + db) % N
        return device(x, bb + c * (aa - bb), aa + c * (bb - aa), c)

    sibling = device(x, y, z, 1 - c)
    left, right = device((x + 3) % N, y, z, c), device((x + 1) % N, y, z, c)

    def piece(dx, cc, start, size):
        xx = (x + dx) % N
        first = ((xx % 2) * 2 + cc) * CROWS + start
        return chans.at[xx // 2, pl.ds(pl.multiple_of(first, HCH), size)]

    loads = (
        pltpu.make_async_copy(tgt_hbm, piece(0, c, 0, CROWS), in_sems.at[0]),
        pltpu.make_async_copy(proj_hbm, proj_ref, in_sems.at[1]),
        pltpu.make_async_copy(src_hbm, src_ref, in_sems.at[2]),
    )
    for load in loads:
        load.start()
    barrier = pltpu.get_barrier_semaphore()
    others = [(k, 0) for k in range(1, N)] + [(0, k) for k in range(1, N)]
    for other in (left, right, sibling):
        pl.semaphore_signal(barrier, inc=1, device_id=other, device_id_type=MESH)
    for da, db in others:
        pl.semaphore_signal(barrier, inc=1, device_id=peer(da, db), device_id_type=MESH)
    pl.semaphore_wait(barrier, 3 + len(others))

    def remote(src, dst, send_sem, recv_sem, other):
        return pltpu.make_async_remote_copy(
            src_ref=src,
            dst_ref=dst,
            send_sem=send_sem,
            recv_sem=recv_sem,
            device_id=other,
            device_id_type=MESH,
        )

    def ring_copy(k, arrival):
        step, owner, h = RING[k]
        ref = piece(owner - step * arrival + N, c, h * HCH, HCH)
        fresh = owner == 0 and not arrival
        src = tgt_hbm.at[pl.ds(h * HCH, HCH)] if fresh else ref
        return remote(src, ref, p_send.at[k], p_recv.at[k], right if step == 1 else left)

    def core_copy(k, arrival):
        cc = 1 - c if arrival else c
        if k == len(RING):
            ref = piece(0, cc, 0, CROWS)
        else:
            step, owner, h = RING[k]
            ref = piece(owner - step + N, cc, h * HCH, HCH)
        src = tgt_hbm if k == len(RING) and not arrival else ref
        return remote(src, ref, f_send.at[k], f_recv.at[k], sibling)

    def q_block(k, arrival):
        ref = qbuf.at[b * N + (a + (N - k if arrival else 0)) % N]
        return remote(ref, ref, q1_send.at[k], q1_recv.at[k], peer(k, 0))

    def q_cross(v, k, arrival):
        row = (b + (N - v if arrival else 0)) % N
        ref = qbuf.at[row * N + (a + N - k) % N]
        i = v * N + k
        return remote(ref, ref, q2_send.at[i], q2_recv.at[i], peer(0, v))

    def feat_copy(r, j):
        i = r * N + j
        return remote(stage.at[i], inbox.at[i], o_send.at[i], o_recv.at[i], peer(j, 0))

    def relay_feat(r):
        return remote(rout.at[r], rin.at[r], ro_send.at[r], ro_recv.at[r], peer(0, r))

    for k in range(4):
        ring_copy(k, False).start()
    core_copy(6, False).start()

    for load in loads:
        load.wait()
    queries = jnp.dot(src_ref[...], proj_ref[...], preferred_element_type=F32).astype(BF16)
    qbuf[b * N + a] = (queries.astype(F32) * (1.0 / 16.0)).astype(BF16)
    for k in (1, 3, 2):
        q_block(k, False).start()

    def pass_on(k):
        for v in (2, 1, 3):
            q_cross(v, k, False).start()

    pass_on(0)

    mine = x // 2
    col = lax.broadcasted_iota(jnp.int32, (1, STRIP), 1)
    row = lax.broadcasted_iota(jnp.int32, (AUG, STRIP), 0)
    for e in range(2):
        strip = mine if e == 0 else 1 - mine
        base = ((y * 2 + strip) * 4 + z) * STRIP
        kx, ky = grid_of((base + col).astype(F32))
        kxh = jnp.floor(kx * (1.0 / 16.0))
        kxl = kx - 16.0 * kxh
        aug = jnp.where(
            row == 0,
            1.0,
            jnp.where(row == 1, kxh, jnp.where(row == 2, kxl, jnp.where(row == 3, ky, 0.0))),
        )
        keys_t[e, C : C + AUG, :] = aug.astype(BF16)

    def project(e):
        block = chans[mine if e == 0 else 1 - mine]
        keys[e] = lax.dot_general(block, proj_ref[...], TN, preferred_element_type=F32).astype(BF16)

    def project_turned(e):
        block = chans[mine if e == 0 else 1 - mine]
        keys_t[e, 0:C, :] = lax.dot_general(
            proj_ref[...], block, TN, preferred_element_type=F32
        ).astype(BF16)

    for k in (1, 3):
        q_block(k, True).wait_recv()
        pass_on(k)
    for k in range(2):
        ring_copy(k, True).wait_recv()
        ring_copy(k + 4, False).start()
        core_copy(k, False).start()
    q_block(2, True).wait_recv()
    pass_on(2)
    for k in range(2, 4):
        ring_copy(k, True).wait_recv()
        core_copy(k, False).start()
    for k in (6, 0, 1, 2, 3):
        core_copy(k, True).wait_recv()
    project(0)
    for k in range(4, 6):
        ring_copy(k, True).wait_recv()
        core_copy(k, False).start()

    def relay(r):
        for j in range(1, N):
            feat_copy(r, j).wait_recv()
        i = r * N
        top, feat, stat = merge(
            [whole(stage[i])] + [whole(inbox[i + j]) for j in range(1, N)]
        )
        srow = lax.broadcasted_iota(jnp.int32, (8, ROWS), 0)
        rout[r, 0:C] = feat.astype(BF16)
        rout[r, C:PACKED] = spread(jnp.where(srow == TOP, top, stat))
        relay_feat(r).start()

    def apart(body):
        def once(_, carry):
            body()
            return carry

        lax.fori_loop(b, b + 1, once, 0)

    def block(t, e):
        i = 2 * t + e
        return offset(0, i), offset(1, i)

    def await_queries(t):
        for e in range(2):
            r, j = block(t, e)

            @pl.when(r > 0)
            def _():
                q_cross(N - r, (N - j) % N, True).wait_recv()

    def query_pair(t):
        pair = []
        for e in range(2):
            r, j = block(t, e)
            pair.append(qbuf[((b + r) % N) * N + (a + j) % N])
        return jnp.concatenate(pair, axis=0)

    def emit(t, o, m):
        srow = lax.broadcasted_iota(jnp.int32, (8, 2 * ROWS), 0)
        stat = spread(jnp.where(srow == TOP, m, o[C : C + 8, :]))
        for e in range(2):
            r, j = block(t, e)
            lanes = slice(e * ROWS, (e + 1) * ROWS)
            stage[r * N + j, 0:C] = o[:C, lanes].astype(BF16)
            stage[r * N + j, C:PACKED] = stat[:, lanes]

            @pl.when(j > 0)
            def _():
                feat_copy(r, j).start()

    def step(t, slot, matching, gathering):
        def body():
            if matching:
                q = query_pair(t + 1)
            if gathering:
                m = top_ref[slot]
            tops, parts = [], []
            for e in range(2):
                if matching:
                    s = lax.dot_general(keys[e], q, NT, preferred_element_type=F32)
                    (scores_b, scores_a)[slot][e] = s
                    tops.append(jnp.max(s, axis=0, keepdims=True))
                if gathering:
                    w = jnp.exp((scores_a, scores_b)[slot][e] - m).astype(BF16)
                    parts.append(jnp.dot(keys_t[e], w, preferred_element_type=F32))
            if matching:
                top_ref[1 - slot] = jnp.maximum(tops[0], tops[1])
            if gathering:
                emit(t, parts[0] + parts[1], m)

        apart(body)

    def first_match(e):
        def body():
            s = lax.dot_general(keys[e], query_pair(0), NT, preferred_element_type=F32)
            scores_a[e] = s
            top = jnp.max(s, axis=0, keepdims=True)
            top_ref[0] = top if e == 0 else jnp.maximum(top_ref[0], top)
            project_turned(e)

        apart(body)

    def two_turns(u, carry):
        await_queries(2 * u + 1)
        step(2 * u, 0, True, True)

        await_queries(2 * u + 2)
        step(2 * u + 1, 1, True, True)
        return carry

    await_queries(0)
    first_match(0)
    for k in range(4, 6):
        core_copy(k, True).wait_recv()
    project(1)
    first_match(1)
    lax.fori_loop(0, N - 1, two_turns, 0)
    relay(2)
    await_queries(2 * N - 1)
    step(2 * N - 2, 0, True, True)
    step(2 * N - 1, 1, False, True)
    relay(1)
    relay(3)

    def await_block(r, j):
        feat_copy(r, j).wait_recv()

    def await_relay(r):
        relay_feat(r).wait_recv()

    for j in (2, 1):
        await_block(0, j)
    await_relay(2)
    top, feats, total = merge(
        [whole(stage[0]), whole(inbox[2]), whole(inbox[1]), whole(rin[2])]
    )
    trow = lax.broadcasted_iota(jnp.int32, (8, ROWS), 0)
    await_block(0, 3)
    for r in (1, 3):
        await_relay(r)
    _, feats, total = merge(
        [(feats, jnp.where(trow == TOP, top, total))]
        + [whole(block) for block in (inbox[3], rin[1], rin[3])]
    )
    inv = 1.0 / total[0:1]
    s_idx, t_idx = lax.axis_index("src"), lax.axis_index("tgt")
    lane = lax.broadcasted_iota(jnp.int32, (1, ROWS), 1)
    ox, oy = grid_of(((s_idx * 32 + t_idx) * ROWS + lane).astype(F32))
    cx = (total[1:2] * 16.0 + total[2:3]) * inv
    cy = total[3:4] * inv
    flow_ref[0:1, :] = (cx - ox) * (1.0 / W_GRID)
    flow_ref[1:2, :] = (cy - oy) * (1.0 / W_GRID)
    matched_ref[...] = (feats * inv).T.astype(BF16)

    for k in range(6):
        ring_copy(k, False).wait_send()
    for k in range(7):
        core_copy(k, False).wait_send()
    for k in range(1, N):
        q_block(k, False).wait_send()
    for r in range(1, N):
        relay_feat(r).wait_send()

    def settle(i, carry):
        r, j = i // N, i % N

        @pl.when(r > 0)
        def _():
            q_cross(r, j, False).wait_send()

        @pl.when(j > 0)
        def _():
            feat_copy(r, j).wait_send()

        return carry

    lax.fori_loop(0, GROUP, settle, 0)


def per_device(source_feat, target_feat, proj):
    dma = pltpu.SemaphoreType.DMA
    vmem = pl.BlockSpec(memory_space=pltpu.VMEM)
    args = (source_feat, target_feat.T, proj)
    return pl.pallas_call(
        kernel,
        out_shape=(
            jax.ShapeDtypeStruct((2, ROWS), F32),
            jax.ShapeDtypeStruct((ROWS, C), BF16),
        ),
        in_specs=[pl.BlockSpec(memory_space=pltpu.HBM)] * 3,
        out_specs=[vmem] * 2,
        scratch_shapes=[
            pltpu.VMEM((ROWS, C), BF16),
            pltpu.VMEM((C, C), BF16),
            pltpu.VMEM((2, C, STRIP), BF16),
            pltpu.VMEM((GROUP, ROWS, C), BF16),
            pltpu.VMEM((2, STRIP, C), BF16),
            pltpu.VMEM((2, C + AUG, STRIP), BF16),
            pltpu.VMEM((2, STRIP, 2 * ROWS), F32),
            pltpu.VMEM((2, STRIP, 2 * ROWS), F32),
            pltpu.VMEM((2, 1, 2 * ROWS), F32),
            pltpu.VMEM((GROUP, PACKED, ROWS), BF16),
            pltpu.VMEM((GROUP, PACKED, ROWS), BF16),
            pltpu.VMEM((N, PACKED, ROWS), BF16),
            pltpu.VMEM((N, PACKED, ROWS), BF16),
            dma((3,)),
            dma((6,)),
            dma((6,)),
            dma((7,)),
            dma((7,)),
            dma((N,)),
            dma((N,)),
            dma((GROUP,)),
            dma((GROUP,)),
            dma((GROUP,)),
            dma((GROUP,)),
            dma((N,)),
            dma((N,)),
        ],
        compiler_params=pltpu.CompilerParams(
            collective_id=0, has_side_effects=True, vmem_limit_bytes=50 << 20
        ),
        name="match_kernel",
    )(*(pltpu.with_memory_space_constraint(arg, pltpu.HBM) for arg in args))


def solution(mesh):
    in_specs = (P(("src", "tgt"), None), P("tgt", "src"), P())
    out_specs = (P(None, ("src", "tgt")), P(("src", "tgt"), None))
    return jax.shard_map(
        per_device, mesh=mesh, in_specs=in_specs, out_specs=out_specs, check_vma=False
    )
```
